32 devices in a mesh: groups: 2 (over y), coord: 16 (over z, x, core).
Axes of the slice: x: 2, y: 2, z: 4, core: 2. Of those that a mesh axis runs over, the one named last changes fastest.
Arguments:
- activations: bfloat16 [64, 128, 4096], P(('groups', 'coord')), parts along dimension 0, may hold values from -6 to 6
- out_grads: bfloat16 [64, 128, 4096], P(('groups', 'coord')), parts along dimension 0, may hold values from -6 to 6
- proj_in: bfloat16 [4096, 128], P('coord'), may hold values from -0.09375 to 0.09375
- proj_out: bfloat16 [4096, 128], P('coord'), may hold values from -0.09375 to 0.09375
- cov_in: float32 [128, 128], replicated
- cov_out: float32 [128, 128], replicated
- lengths: int32 [64], P(('groups', 'coord')), parts along dimension 0, may hold values from 1 to 128
- seq_ids: int32 [64], P(('groups', 'coord')), parts along dimension 0, may hold values from 0 to 31, each once
- bank: bfloat16 [1536, 16384], P(None, 'coord'), may hold values from -0.015625 to 0.015625
Outputs:
- scores: bfloat16 [64, 1536], P('groups', 'coord'), parts along dimension 0
The draws below stay inside these ranges and needn't reach their ends.
There are 2 independent parts, one for each index of `groups`. The reference program is written for one: setup_inputs(seed, part) draws one part's arguments, and reference() takes and returns one part's arrays. A program takes and returns all parts, laid end to end along the dimension named above; an argument that names none is the same for every part. Nothing has to cross between parts.
All inputs are finite; a program needn't handle non-finite values.
Results may differ from the reference program's by a relative error of at most 0.0064.
Values may be sent and summed in bfloat16 or wider, within the bound.
A program may use at most 128 MiB of HBM per device.

```python
import math
import jax
import jax.numpy as jnp
from jax import lax

D = 4096
RANK = 128
LEN = 128
SEQS = 32
QUERIES = 1536
COORDS = 16384


def make_factor(key):
    first, second = jax.random.split(key)
    mixing = jax.random.normal(first, (RANK, RANK), jnp.float32)
    lower_end, upper_end = (0.5, 5.0)
    diagonal = jnp.exp(jax.random.uniform(second, (RANK,), jnp.float32, math.log(lower_end), math.log(upper_end)))
    factor = jnp.dot(mixing, mixing.T) / RANK + jnp.diag(diagonal)
    return 0.5 * (factor + factor.T)


def draw_cov_in(key, part):
    return make_factor(jax.random.fold_in(key, 21))


def draw_cov_out(key, part):
    return make_factor(jax.random.fold_in(key, 37))


def draw_lengths(key, part):
    values = jax.random.randint(jax.random.fold_in(key, 5), (SEQS,), 1, LEN + 1)
    return values.at[0].set(LEN).at[1].set(1).astype(jnp.int32)


def strengthened(result, key, source, target, blocks, factor):
    def block_of(axis_at):
        return (jnp.arange(result.shape[axis_at]) // (result.shape[axis_at] // blocks)).reshape((-1,) + (1,) * (result.ndim - 1 - axis_at))

    one_side = jax.random.permutation(key, blocks)[block_of(target)]
    far = (block_of(target) + blocks // 2) % blocks
    return jnp.where((block_of(source) == one_side) | (block_of(source) == far), factor * result, result)


def shard_levels(stream_key, extent, shards, smallest, largest):
    factor_of, own = 1.0, jax.random.fold_in(stream_key, 6)
    for dim, parts in shards:
        steps = jnp.exp(jax.random.uniform(jax.random.fold_in(own, dim), (parts,), jnp.float32, smallest / len(shards), largest / len(shards)))
        factor_of = factor_of * jnp.repeat(steps, extent[dim] // parts).reshape([-1 if axis == dim else 1 for axis in range(len(extent))])
    return factor_of


def scatter_about(stream_key, extent, scale, bound, cuts=(), held_as=jnp.bfloat16):
    array = jax.random.normal(stream_key, extent, jnp.float32) * scale
    if len(cuts) > 0:
        array = shard_levels(stream_key, extent, cuts, -0.22, 0.18) * array
    return jnp.clip(array, min=-bound, max=bound).astype(held_as)


def heavy_noise(own_key, shape, scale, reach, cuts, heavy, held_as=jnp.bfloat16):
    values = scale * jax.random.normal(own_key, shape, jnp.float32)
    if cuts:
        values = values * shard_levels(own_key, shape, cuts, -0.22, 0.18)
    return jnp.clip(strengthened(values, jax.random.fold_in(own_key, 3), *heavy), -reach, reach).astype(held_as)


def setup_inputs(seed: int = 0, part: int = 0) -> dict:
    seeds = jax.random.split(jax.random.key(seed), 10)
    own_keys = jax.random.split(jax.random.fold_in(seeds[9], part), 10)
    activations = scatter_about(own_keys[0], (SEQS, LEN, D), 1.0, 6.0, ((0, 16),))
    out_grads = scatter_about(own_keys[1], (SEQS, LEN, D), 1.0, 6.0, ((0, 16),))
    proj_in = scatter_about(seeds[2], (D, RANK), D ** -0.5, 0.09375, ((0, 16),))
    proj_out = scatter_about(seeds[3], (D, RANK), D ** -0.5, 0.09375, ((0, 16),))
    cov_in = draw_cov_in(jax.random.fold_in(seeds[9], 71), part)
    cov_out = draw_cov_out(jax.random.fold_in(seeds[9], 71), part)
    lengths = draw_lengths(jax.random.fold_in(jax.random.fold_in(seeds[9], part), 71), part)
    seq_ids = jax.random.permutation(own_keys[7], SEQS).astype(jnp.int32)
    bank = heavy_noise(seeds[8], (QUERIES, COORDS), (COORDS * 16) ** -0.5, 0.015625, ((1, 16),), (1, 0, 16, 2.0))
    return {"activations": activations, "out_grads": out_grads, "proj_in": proj_in, "proj_out": proj_out, "cov_in": cov_in, "cov_out": cov_out, "lengths": lengths, "seq_ids": seq_ids, "bank": bank}


def inverse_factor(cov):
    size = cov.shape[0]
    damping = 0.1 * jnp.trace(cov) / size
    eye = jnp.eye(size, dtype=jnp.float32)
    lower = jnp.linalg.cholesky(cov + damping * eye)
    return jax.scipy.linalg.cho_solve((lower, True), eye)

def reference(activations, out_grads, proj_in, proj_out, cov_in, cov_out, lengths, seq_ids, bank):
    seqs, length, width = activations.shape
    rank = proj_in.shape[1]
    x_full = jnp.dot(activations.reshape(seqs * length, width).astype(jnp.float32), proj_in.astype(jnp.float32), preferred_element_type=jnp.float32).reshape(seqs, length, rank)
    position = lax.broadcasted_iota(jnp.int32, (seqs, length), 1)
    valid = (position < lengths[:, None]).astype(jnp.float32)
    x_proj = (x_full * valid[:, :, None]).astype(jnp.bfloat16)
    d_proj = jnp.dot(out_grads.reshape(seqs * length, width).astype(jnp.float32), proj_out.astype(jnp.float32), preferred_element_type=jnp.float32).reshape(seqs, length, rank).astype(jnp.bfloat16)
    grads = jnp.einsum('sto,sti->soi', d_proj.astype(jnp.float32), x_proj.astype(jnp.float32), preferred_element_type=jnp.float32)
    k_in = inverse_factor(cov_in)
    k_out = inverse_factor(cov_out)
    left = jnp.einsum('ab,sbc->sac', k_out, grads, precision=lax.Precision.HIGHEST)
    whitened = jnp.einsum('sac,cd->sad', left, k_in, precision=lax.Precision.HIGHEST)
    whitened = whitened.astype(jnp.bfloat16).reshape(seqs, rank * rank)
    raw = lax.dot_general(whitened.astype(jnp.float32), bank.astype(jnp.float32), (((1,), (1,)), ((), ())), preferred_element_type=jnp.float32).astype(jnp.bfloat16)
    return jnp.zeros_like(raw).at[seq_ids].set(raw)
```

```python
import functools

import jax
import jax.numpy as jnp
from jax import lax
from jax.experimental import pallas as pl
from jax.experimental.pallas import tpu as pltpu
from jax.sharding import PartitionSpec as P

MESH = pl.DeviceIdType.MESH
F32 = jnp.float32
BF16 = jnp.bfloat16
PANEL = 8


def xor(value, mask):
    bit = 1
    result = value
    while bit <= mask:
        if mask & bit:
            result = result + bit - 2 * bit * ((value // bit) % 2)
        bit *= 2
    return result


def start_factor(cov):
    size = cov.shape[0]
    rows = lax.broadcasted_iota(jnp.int32, (size, size), 0)
    lanes = lax.broadcasted_iota(jnp.int32, (size, size), 1)
    diagonal = jnp.where(rows == lanes, cov, 0.0)
    damping = 0.1 * jnp.sum(diagonal) / size
    return jnp.where(rows == lanes, cov + damping, cov)


def eliminate_panel(matrix):
    size = matrix.shape[0]
    top, rest = matrix[:PANEL], matrix[PANEL:]
    lane = lax.broadcasted_iota(jnp.int32, (1, size), 1)
    sub = lax.broadcasted_iota(jnp.int32, (PANEL, 1), 0)
    for r in range(PANEL):
        row = top[r : r + 1]
        inverse = 1.0 / row[:, r : r + 1]
        scaled = jnp.where(lane == r, inverse, row * inverse)
        top_new = jnp.where(lane == r, 0.0, top) - top[:, r : r + 1] * scaled
        rest = jnp.where(lane == r, 0.0, rest) - rest[:, r : r + 1] * scaled
        top = jnp.where(sub == r, scaled, top_new)
    whole = jnp.concatenate([rest, top], axis=0)
    return pltpu.roll(whole, size - PANEL, 1)


def kernel(
    n, slow, fast,
    act_ref, og_ref, pin_ref, pout_ref, cin_ref, cout_ref, len_ref, ids_ref, bank_ref,
    out_ref,
    act, og, bank, g, k, idbuf, wsend, wrecv, psend, precv,
    load_sem, gs_sem, gr_sem, is_sem, ir_sem, ws_sem, wr_sem, ps_sem, pr_sem,
):
    group = lax.axis_index("groups")
    me = lax.axis_index("coord")
    seqs = len_ref.shape[0]
    length = act.shape[0] // seqs
    rank = cin_ref.shape[0]
    shard = pin_ref.shape[0]
    queries = out_ref.shape[1]
    per = bank_ref.shape[1] // rank
    block = wsend.shape[1]

    loads = [
        pltpu.make_async_copy(pin_ref, g.at[me, 0], load_sem.at[0]),
        pltpu.make_async_copy(pout_ref, g.at[me, 1], load_sem.at[1]),
        pltpu.make_async_copy(act_ref, act, load_sem.at[2]),
        pltpu.make_async_copy(og_ref, og, load_sem.at[3]),
        pltpu.make_async_copy(bank_ref, bank.at[pl.ds(0, bank_ref.shape[0])], load_sem.at[4]),
    ]
    for load in loads:
        load.start()

    barrier = pltpu.get_barrier_semaphore()
    for j in range(1, n):
        pl.semaphore_signal(barrier, inc=1, device_id=(group, xor(me, j)), device_id_type=MESH)

    for s in range(seqs):
        idbuf[me, s : s + 1] = jnp.full((1, idbuf.shape[2]), ids_ref[s], jnp.int32)
    k[0] = start_factor(cin_ref[...])
    k[1] = start_factor(cout_ref[...])
    tail = bank.shape[0] - bank_ref.shape[0]
    if tail:
        bank[bank_ref.shape[0] :] = jnp.zeros((tail, bank.shape[1]), BF16)
    if block > seqs * per:
        wsend[...] = jnp.zeros_like(wsend)

    loads[0].wait()
    loads[1].wait()
    pl.semaphore_wait(barrier, n - 1)

    gathers = []

    def send(slot_mask, to_mask):
        slot = xor(me, slot_mask)
        copy = pltpu.make_async_remote_copy(
            src_ref=g.at[slot], dst_ref=g.at[slot],
            send_sem=gs_sem.at[len(gathers)], recv_sem=gr_sem.at[slot],
            device_id=(group, xor(me, to_mask)), device_id_type=MESH,
        )
        copy.start()
        gathers.append(copy)

    def arrived(slot_mask):
        slot = xor(me, slot_mask)
        pltpu.make_async_remote_copy(
            src_ref=g.at[slot], dst_ref=g.at[slot],
            send_sem=gs_sem.at[0], recv_sem=gr_sem.at[slot],
            device_id=(group, xor(me, 1)), device_id_type=MESH,
        ).wait_recv()

    fasts = [2 * b for b in range(1, fast)]
    slows = [2 * fast * a for a in range(1, slow)]
    for mask in fasts + slows:
        send(0, mask)
    send(0, 1)

    id_copies = []
    for j in range(1, n):
        copy = pltpu.make_async_remote_copy(
            src_ref=idbuf.at[me], dst_ref=idbuf.at[me],
            send_sem=is_sem.at[j], recv_sem=ir_sem.at[j],
            device_id=(group, xor(me, j)), device_id_type=MESH,
        )
        copy.start()
        id_copies.append(copy)

    def from_slow(mask):
        arrived(mask)
        for b in fasts:
            send(mask, b)
        send(mask, 1)

    def from_fast(mask):
        for b in fasts:
            arrived(mask + b)
            send(mask + b, 1)

    events = []
    for a in range(slow):
        if a + 1 < slow:
            events.append((from_slow, slows[a]))
        events.append((from_fast, slows[a - 1] if a else 0))

    panels = rank // PANEL

    def step(_, carry):
        first, second = k[0], k[1]
        k[0] = eliminate_panel(first)
        k[1] = eliminate_panel(second)
        return carry

    done = 0
    for at, (event, mask) in enumerate(events):
        upto = panels * (at + 1) // len(events)
        if upto > done:
            lax.fori_loop(0, upto - done, step, 0)
            done = upto
        event(mask)

    loads[2].wait()
    loads[3].wait()
    for mask in [0] + slows:
        for b in [0] + fasts:
            arrived(mask + b + 1)

    join = max(1, 256 // shard)
    x_full = jnp.zeros((seqs * length, rank), F32)
    d_full = jnp.zeros((seqs * length, rank), F32)
    for o in range(0, n, join):
        columns = slice(o * shard, (o + join) * shard)
        x_full += jnp.dot(
            act[:, columns], g[o : o + join, 0].reshape(join * shard, rank), preferred_element_type=F32
        )
        d_full += jnp.dot(
            og[:, columns], g[o : o + join, 1].reshape(join * shard, rank), preferred_element_type=F32
        )
    position = lax.broadcasted_iota(jnp.int32, (length, 1), 0)
    for s in range(seqs):
        rows = slice(s * length, (s + 1) * length)
        valid = (position < len_ref[s]).astype(F32)
        x_proj = (x_full[rows] * valid).astype(BF16)
        d_proj = d_full[rows].astype(BF16)
        grads = lax.dot_general(d_proj, x_proj, (((0,), (0,)), ((), ())), preferred_element_type=F32)
        left = jnp.dot(k[1], grads, precision=lax.Precision.HIGHEST, preferred_element_type=F32)
        white = jnp.dot(left, k[0], precision=lax.Precision.HIGHEST, preferred_element_type=F32)
        wsend[:, s * per : (s + 1) * per] = white.reshape(n, per, rank)

    def exchange(src, dst, send_sem, recv_sem, j):
        copy = pltpu.make_async_remote_copy(
            src_ref=src, dst_ref=dst,
            send_sem=send_sem.at[j], recv_sem=recv_sem.at[j],
            device_id=(group, xor(me, j)), device_id_type=MESH,
        )
        copy.start()
        return copy

    mine = pl.ds(pl.multiple_of(me * block, block), block)
    white_copies = [
        exchange(wsend.at[xor(me, j)], wrecv.at[mine], ws_sem, wr_sem, j) for j in range(n - 1, 0, -1)
    ]
    wrecv[mine] = wsend[me]
    loads[4].wait()
    for copy in white_copies:
        copy.wait_recv()
    for copy in id_copies:
        copy.wait_recv()

    columns = jnp.concatenate(
        [
            jnp.concatenate(
                [wrecv[pl.ds(s * per + a, n, stride=block), :] for s in range(seqs)], axis=0
            ).astype(BF16)
            for a in range(per)
        ],
        axis=1,
    )

    def partial(target):
        rows = bank[pl.ds(pl.multiple_of(target * queries, queries), psend.shape[2])]
        return lax.dot_general(columns, rows, (((1,), (1,)), ((), ())), preferred_element_type=F32)

    score_copies = []
    for j in range(n - 1, 0, -1):
        psend[j] = partial(xor(me, j)).astype(BF16)
        score_copies.append(exchange(psend.at[j], precv.at[j], ps_sem, pr_sem, j))
    total = partial(me)
    ids = jnp.concatenate([idbuf[:, s, :] for s in range(seqs)], axis=0)[:, :1]
    held = n * seqs
    one_hot = (ids == lax.broadcasted_iota(jnp.int32, (held, held), 1)).astype(BF16)
    for copy in score_copies:
        copy.wait_recv()
    for j in range(n - 1, 0, -1):
        total += precv[j].astype(F32)
    placed = lax.dot_general(
        one_hot, total.astype(BF16), (((0,), (0,)), ((), ())), preferred_element_type=F32
    )
    out_ref[...] = placed[:, :queries].astype(BF16)
    for copy in gathers + id_copies + white_copies + score_copies:
        copy.wait_send()


def solution(mesh):
    n = mesh.shape["coord"]
    chips = n // 2
    slow = 1
    while slow * slow < chips:
        slow *= 2
    fast = chips // slow

    def body(activations, out_grads, proj_in, proj_out, cov_in, cov_out, lengths, seq_ids, bank):
        seqs, length, width = activations.shape
        shard, rank = proj_in.shape
        per = bank.shape[1] // rank
        queries = bank.shape[0] // n
        wide = -(-queries // 128) * 128
        block = -(-(seqs * per) // 8) * 8
        held = n * seqs
        vmem = pl.BlockSpec(memory_space=pltpu.VMEM)
        smem = pl.BlockSpec(memory_space=pltpu.SMEM)
        hbm = pl.BlockSpec(memory_space=pl.ANY)
        dma = pltpu.SemaphoreType.DMA
        return pl.pallas_call(
            functools.partial(kernel, n, slow, fast),
            out_shape=jax.ShapeDtypeStruct((held, queries), BF16),
            in_specs=[hbm, hbm, hbm, hbm, vmem, vmem, smem, smem, hbm],
            out_specs=vmem,
            scratch_shapes=[
                pltpu.VMEM((seqs * length, width), BF16),
                pltpu.VMEM((seqs * length, width), BF16),
                pltpu.VMEM((bank.shape[0] + wide - queries, bank.shape[1]), BF16),
                pltpu.VMEM((n, 2, shard, rank), BF16),
                pltpu.VMEM((2, rank, rank), F32),
                pltpu.VMEM((n, seqs, 128), jnp.int32),
                pltpu.VMEM((n, block, rank), F32),
                pltpu.VMEM((n * block, rank), F32),
                pltpu.VMEM((n, held, wide), BF16),
                pltpu.VMEM((n, held, wide), BF16),
                dma((5,)),
                dma((n,)), dma((n,)), dma((n,)), dma((n,)),
                dma((n,)), dma((n,)), dma((n,)), dma((n,)),
            ],
            compiler_params=pltpu.CompilerParams(collective_id=0, has_side_effects=True),
        )(
            activations.reshape(seqs * length, width), out_grads.reshape(seqs * length, width),
            proj_in, proj_out, cov_in, cov_out, lengths, seq_ids, bank,
        )

    in_specs = (
        P(("groups", "coord"), None, None),
        P(("groups", "coord"), None, None),
        P("coord", None),
        P("coord", None),
        P(),
        P(),
        P(("groups", "coord")),
        P(("groups", "coord")),
        P(None, "coord"),
    )
    return jax.shard_map(body, mesh=mesh, in_specs=in_specs, out_specs=P("groups", "coord"), check_vma=False)
```

```python
import functools

import jax
import jax.numpy as jnp
from jax import lax
from jax.experimental import pallas as pl
from jax.experimental.pallas import tpu as pltpu
from jax.sharding import PartitionSpec as P

MESH = pl.DeviceIdType.MESH
F32 = jnp.float32
BF16 = jnp.bfloat16
PANEL = 8


def xor(value, mask):
    bit = 1
    result = value
    while bit <= mask:
        if mask & bit:
            result = result + bit - 2 * bit * ((value // bit) % 2)
        bit *= 2
    return result


def start_factor(cov):
    size = cov.shape[0]
    rows = lax.broadcasted_iota(jnp.int32, (size, size), 0)
    lanes = lax.broadcasted_iota(jnp.int32, (size, size), 1)
    diagonal = jnp.where(rows == lanes, cov, 0.0)
    damping = 0.1 * jnp.sum(diagonal) / size
    return jnp.where(rows == lanes, cov + damping, cov)


def eliminate_panel(matrix):
    size = matrix.shape[0]
    top, rest = matrix[:PANEL], matrix[PANEL:]
    lane = lax.broadcasted_iota(jnp.int32, (PANEL, size), 1)
    sub = lax.broadcasted_iota(jnp.int32, (PANEL, size), 0)
    pivots = [jnp.broadcast_to(top[:, r : r + 1], (PANEL, size)) for r in range(PANEL)]
    top = jnp.where(lane < PANEL, jnp.where(lane == sub, 1.0, 0.0), top)
    for r in range(PANEL):
        factor = pivots[r]
        inverse = 1.0 / factor[r : r + 1]

        def reduced(value):
            scaled = value[r : r + 1] * inverse
            return jnp.where(sub == r, scaled, value - factor * scaled)

        top = reduced(top)
        for later in range(r + 1, PANEL):
            pivots[later] = reduced(pivots[later])
    column = rest
    rest = jnp.where(lane[:1] < PANEL, 0.0, rest)
    for r in range(PANEL):
        rest = rest - column[:, r : r + 1] * top[r : r + 1]
    whole = jnp.concatenate([rest, top], axis=0)
    return pltpu.roll(whole, size - PANEL, 1)


def kernel(
    n, slow, fast,
    act_ref, og_ref, pin_ref, pout_ref, cin_ref, cout_ref, len_hbm, ids_hbm, bank_ref,
    out_ref, len_ref, ids_ref,
    act, og, bank, g, k, x_full, d_full, idbuf, wsend, wrecv, psend, precv,
    load_sem, gs_sem, gr_sem, is_sem, ir_sem, ws_sem, wr_sem, ps_sem, pr_sem,
):
    group = lax.axis_index("groups")
    me = lax.axis_index("coord")
    seqs = len_ref.shape[0]
    length = act.shape[0] // seqs
    rank = cin_ref.shape[0]
    shard = pin_ref.shape[0]
    queries = out_ref.shape[1]
    per = bank_ref.shape[1] // rank
    block = wsend.shape[1]

    loads = [
        pltpu.make_async_copy(pin_ref, g.at[me, 0], load_sem.at[0]),
        pltpu.make_async_copy(pout_ref, g.at[me, 1], load_sem.at[1]),
        pltpu.make_async_copy(act_ref, act, load_sem.at[2]),
        pltpu.make_async_copy(og_ref, og, load_sem.at[3]),
        pltpu.make_async_copy(bank_ref, bank.at[pl.ds(0, bank_ref.shape[0])], load_sem.at[4]),
        pltpu.make_async_copy(cin_ref, k.at[0], load_sem.at[5]),
        pltpu.make_async_copy(cout_ref, k.at[1], load_sem.at[6]),
        pltpu.make_async_copy(len_hbm, len_ref, load_sem.at[7]),
        pltpu.make_async_copy(ids_hbm, ids_ref, load_sem.at[8]),
    ]
    for load in loads[:2] + loads[5:] + loads[2:5]:
        load.start()

    barrier = pltpu.get_barrier_semaphore()
    pl.semaphore_signal(barrier, inc=1, device_id=(1 - group, me), device_id_type=MESH)
    for j in range(1, n):
        pl.semaphore_signal(barrier, inc=1, device_id=(group, xor(me, j)), device_id_type=MESH)

    loads[0].wait()
    loads[1].wait()
    pl.semaphore_wait(barrier, n)

    gathers = []
    own, other = group, 1 - group

    def send(slot_mask, piece, to):
        slot = xor(me, slot_mask)
        copy = pltpu.make_async_remote_copy(
            src_ref=g.at[slot, piece], dst_ref=g.at[slot, piece],
            send_sem=gs_sem.at[len(gathers)], recv_sem=gr_sem.at[slot, piece],
            device_id=to, device_id_type=MESH,
        )
        copy.start()
        gathers.append(copy)

    def arrived(slot_mask, piece):
        slot = xor(me, slot_mask)
        pltpu.make_async_remote_copy(
            src_ref=g.at[slot, piece], dst_ref=g.at[slot, piece],
            send_sem=gs_sem.at[0], recv_sem=gr_sem.at[slot, piece],
            device_id=(group, xor(me, 1)), device_id_type=MESH,
        ).wait_recv()

    def peer(mask):
        return (group, xor(me, mask))

    sibling, twin = peer(1), (other, me)
    fasts = [2 * b for b in range(1, fast)]
    slows = [2 * fast * a for a in range(1, slow)]
    early = slows[:1]
    for mask in fasts:
        send(0, own, peer(mask))
    for mask in slows:
        send(0, own, peer(mask))
    for mask in fasts:
        send(0, other, peer(mask))
    send(0, own, sibling)
    send(0, other, sibling)

    for load in loads[5:]:
        load.wait()
    for s in range(seqs):
        idbuf[me, s : s + 1] = jnp.full((1, idbuf.shape[2]), ids_ref[s], jnp.int32)
    k[0] = start_factor(k[0])
    k[1] = start_factor(k[1])
    tail = bank.shape[0] - bank_ref.shape[0]
    if tail:
        bank[bank_ref.shape[0] :] = jnp.zeros((tail, bank.shape[1]), BF16)
    if block > seqs * per:
        wsend[...] = jnp.zeros_like(wsend)

    id_copies = []
    for j in range(1, n):
        copy = pltpu.make_async_remote_copy(
            src_ref=idbuf.at[me], dst_ref=idbuf.at[me],
            send_sem=is_sem.at[j], recv_sem=ir_sem.at[j],
            device_id=(group, xor(me, j)), device_id_type=MESH,
        )
        copy.start()
        id_copies.append(copy)

    def from_slow(mask):
        arrived(mask, own)
        for b in fasts:
            send(mask, own, peer(b))
        send(mask, own, twin)
        send(mask, own, sibling)

    def from_fast(mask):
        for b in fasts:
            arrived(mask + b, own)
            if mask and mask not in early:
                send(mask + b, own, twin)
            send(mask + b, own, sibling)

    def from_twin(mask):
        arrived(mask, other)
        if mask in early:
            for b in fasts:
                send(mask, other, peer(b))
        send(mask, other, sibling)

    def last(mask):
        for b in fasts:
            arrived(mask + b, other)
            send(mask + b, other, sibling)

    span = n // slow * shard

    def project(mask):
        if mask == 0:
            loads[2].wait()
            loads[3].wait()
        for b in [0] + fasts:
            for piece in (own, other):
                arrived(mask + b + 1, piece)
        block_at = xor(me // (2 * fast), mask // (2 * fast))
        columns = pl.ds(pl.multiple_of(block_at * span, 128), span)
        shards = pl.ds(block_at * 2 * fast, 2 * fast)
        x_part = jnp.dot(
            act[:, columns], g[shards, 0].reshape(span, rank), preferred_element_type=F32
        )
        d_part = jnp.dot(
            og[:, columns], g[shards, 1].reshape(span, rank), preferred_element_type=F32
        )
        if mask == 0:
            x_full[...] = x_part
            d_full[...] = d_part
        else:
            x_full[...] += x_part
            d_full[...] += d_part

    events = []
    for a in range(slow):
        if a + 1 < slow:
            events.append((from_slow, slows[a]))
        if a + 2 == slow:
            events.append((project, 0))
        if a:
            events.append((from_twin, slows[a - 1]))
            events.append((from_fast, slows[a - 1]))
            if a > 1:
                events.append((last, slows[a - 2]))
            if a > 2:
                events.append((project, slows[a - 3]))
        else:
            events.append((from_fast, 0))
            if slow > 1:
                events.append((last, 0))
    events.append((last, slows[-1] if slows else 0))
    if slow == 1:
        events.append((project, 0))
    for mask in slows[max(0, slow - 3):]:
        events.append((project, mask))

    panels = rank // PANEL

    def step(_, carry):
        first, second = k[0], k[1]
        k[0] = eliminate_panel(first)
        k[1] = eliminate_panel(second)
        return carry

    done = 0
    for at, (event, mask) in enumerate(events):
        upto = panels * (at + 1) // len(events)
        if upto > done:
            lax.fori_loop(0, upto - done, step, 0)
            done = upto
        event(mask)

    position = lax.broadcasted_iota(jnp.int32, (length, 1), 0)
    for s in range(seqs):
        rows = slice(s * length, (s + 1) * length)
        valid = (position < len_ref[s]).astype(F32)
        x_proj = (x_full[rows] * valid).astype(BF16)
        d_proj = d_full[rows].astype(BF16)
        grads = lax.dot_general(d_proj, x_proj, (((0,), (0,)), ((), ())), preferred_element_type=F32)
        left = jnp.dot(k[1], grads, precision=lax.Precision.HIGHEST, preferred_element_type=F32)
        white = jnp.dot(left, k[0], precision=lax.Precision.HIGHEST, preferred_element_type=F32)
        wsend[:, s * per : (s + 1) * per] = white.reshape(n, per, rank)

    def exchange(src, dst, send_sem, recv_sem, j):
        copy = pltpu.make_async_remote_copy(
            src_ref=src, dst_ref=dst,
            send_sem=send_sem.at[j], recv_sem=recv_sem.at[j],
            device_id=(group, xor(me, j)), device_id_type=MESH,
        )
        copy.start()
        return copy

    mine = pl.ds(pl.multiple_of(me * block, block), block)
    white_copies = [
        exchange(wsend.at[xor(me, j)], wrecv.at[mine], ws_sem, wr_sem, j) for j in range(n - 1, 0, -1)
    ]
    wrecv[mine] = wsend[me]
    loads[4].wait()
    for copy in white_copies:
        copy.wait_recv()
    for copy in id_copies:
        copy.wait_recv()

    columns = jnp.concatenate(
        [
            jnp.concatenate(
                [wrecv[pl.ds(s * per + a, n, stride=block), :] for s in range(seqs)], axis=0
            ).astype(BF16)
            for a in range(per)
        ],
        axis=1,
    )

    def partial(target):
        rows = bank[pl.ds(pl.multiple_of(target * queries, queries), psend.shape[2])]
        return lax.dot_general(columns, rows, (((1,), (1,)), ((), ())), preferred_element_type=F32)

    score_copies = []
    for j in range(n - 1, 0, -1):
        psend[j] = partial(xor(me, j)).astype(BF16)
        score_copies.append(exchange(psend.at[j], precv.at[j], ps_sem, pr_sem, j))
    total = partial(me)
    ids = jnp.concatenate([idbuf[:, s, :] for s in range(seqs)], axis=0)[:, :1]
    held = n * seqs
    one_hot = (ids == lax.broadcasted_iota(jnp.int32, (held, held), 1)).astype(BF16)
    for copy in score_copies:
        copy.wait_recv()
    for j in range(n - 1, 0, -1):
        total += precv[j].astype(F32)
    placed = lax.dot_general(
        one_hot, total.astype(BF16), (((0,), (0,)), ((), ())), preferred_element_type=F32
    )
    out_ref[...] = placed[:, :queries].astype(BF16)
    for copy in gathers + id_copies + white_copies + score_copies:
        copy.wait_send()


def solution(mesh):
    n = mesh.shape["coord"]
    assert mesh.shape["groups"] == 2
    chips = n // 2
    slow = 1
    while slow * slow < chips:
        slow *= 2
    fast = chips // slow

    def body(activations, out_grads, proj_in, proj_out, cov_in, cov_out, lengths, seq_ids, bank):
        seqs, length, width = activations.shape
        shard, rank = proj_in.shape
        per = bank.shape[1] // rank
        queries = bank.shape[0] // n
        wide = -(-queries // 128) * 128
        block = -(-(seqs * per) // 8) * 8
        held = n * seqs
        vmem = pl.BlockSpec(memory_space=pltpu.VMEM)
        hbm = pl.BlockSpec(memory_space=pl.ANY)
        dma = pltpu.SemaphoreType.DMA
        return pl.pallas_call(
            functools.partial(kernel, n, slow, fast),
            out_shape=jax.ShapeDtypeStruct((held, queries), BF16),
            in_specs=[hbm] * 9,
            out_specs=vmem,
            scratch_shapes=[
                pltpu.SMEM((seqs,), jnp.int32),
                pltpu.SMEM((seqs,), jnp.int32),
                pltpu.VMEM((seqs * length, width), BF16),
                pltpu.VMEM((seqs * length, width), BF16),
                pltpu.VMEM((bank.shape[0] + wide - queries, bank.shape[1]), BF16),
                pltpu.VMEM((n, 2, shard, rank), BF16),
                pltpu.VMEM((2, rank, rank), F32),
                pltpu.VMEM((seqs * length, rank), F32),
                pltpu.VMEM((seqs * length, rank), F32),
                pltpu.VMEM((n, seqs, 128), jnp.int32),
                pltpu.VMEM((n, block, rank), F32),
                pltpu.VMEM((n * block, rank), F32),
                pltpu.VMEM((n, held, wide), BF16),
                pltpu.VMEM((n, held, wide), BF16),
                dma((9,)),
                dma((2 * n,)), dma((n, 2)), dma((n,)), dma((n,)),
                dma((n,)), dma((n,)), dma((n,)), dma((n,)),
            ],
            compiler_params=pltpu.CompilerParams(collective_id=0, has_side_effects=True),
        )(
            activations.reshape(seqs * length, width), out_grads.reshape(seqs * length, width),
            proj_in, proj_out, cov_in, cov_out, lengths, seq_ids, bank,
        )

    in_specs = (
        P(("groups", "coord"), None, None),
        P(("groups", "coord"), None, None),
        P("coord", None),
        P("coord", None),
        P(),
        P(),
        P(("groups", "coord")),
        P(("groups", "coord")),
        P(None, "coord"),
    )
    return jax.shard_map(body, mesh=mesh, in_specs=in_specs, out_specs=P("groups", "coord"), check_vma=False)
```

```python
import functools

import jax
import jax.numpy as jnp
from jax import lax
from jax.experimental import pallas as pl
from jax.experimental.pallas import tpu as pltpu
from jax.sharding import PartitionSpec as P

MESH = pl.DeviceIdType.MESH
F32 = jnp.float32
BF16 = jnp.bfloat16
PANEL = 8


def xor(value, mask):
    bit = 1
    result = value
    while bit <= mask:
        if mask & bit:
            result = result + bit - 2 * bit * ((value // bit) % 2)
        bit *= 2
    return result


def start_factor(cov):
    size = cov.shape[0]
    rows = lax.broadcasted_iota(jnp.int32, (size, size), 0)
    lanes = lax.broadcasted_iota(jnp.int32, (size, size), 1)
    diagonal = jnp.where(rows == lanes, cov, 0.0)
    damping = 0.1 * jnp.sum(diagonal) / size
    return jnp.where(rows == lanes, cov + damping, cov)


def eliminate_panel(matrix):
    size = matrix.shape[0]
    top, rest = matrix[:PANEL], matrix[PANEL:]
    lane = lax.broadcasted_iota(jnp.int32, (PANEL, size), 1)
    sub = lax.broadcasted_iota(jnp.int32, (PANEL, size), 0)
    pivots = [jnp.broadcast_to(top[:, r : r + 1], (PANEL, size)) for r in range(PANEL)]
    top = jnp.where(lane < PANEL, jnp.where(lane == sub, 1.0, 0.0), top)
    for r in range(PANEL):
        factor = pivots[r]
        inverse = 1.0 / factor[r : r + 1]

        def reduced(value):
            scaled = value[r : r + 1] * inverse
            return jnp.where(sub == r, scaled, value - factor * scaled)

        top = reduced(top)
        for later in range(r + 1, PANEL):
            pivots[later] = reduced(pivots[later])
    column = rest
    rest = jnp.where(lane[:1] < PANEL, 0.0, rest)
    for r in range(PANEL):
        rest = rest - column[:, r : r + 1] * top[r : r + 1]
    whole = jnp.concatenate([rest, top], axis=0)
    return pltpu.roll(whole, size - PANEL, 1)


def kernel(
    n, slow, fast,
    act_ref, og_ref, pin_ref, pout_ref, cin_ref, cout_ref, len_hbm, ids_hbm, bank_ref,
    out_ref, len_ref, ids_ref,
    act, og, bank, g, k, x_full, d_full, idbuf, wsend, wrecv, psend, precv,
    load_sem, gs_sem, gr_sem, is_sem, ir_sem, ws_sem, wr_sem, ps_sem, pr_sem,
):
    group = lax.axis_index("groups")
    me = lax.axis_index("coord")
    seqs = len_ref.shape[0]
    length = act.shape[0] // seqs
    rank = cin_ref.shape[0]
    shard = pin_ref.shape[0]
    queries = out_ref.shape[1]
    per = bank_ref.shape[1] // rank
    block = wsend.shape[1]

    loads = [
        pltpu.make_async_copy(pin_ref, g.at[me, 0], load_sem.at[0]),
        pltpu.make_async_copy(pout_ref, g.at[me, 1], load_sem.at[1]),
        pltpu.make_async_copy(act_ref, act, load_sem.at[2]),
        pltpu.make_async_copy(og_ref, og, load_sem.at[3]),
        pltpu.make_async_copy(bank_ref, bank.at[pl.ds(0, bank_ref.shape[0])], load_sem.at[4]),
        pltpu.make_async_copy(cin_ref, k.at[0], load_sem.at[5]),
        pltpu.make_async_copy(cout_ref, k.at[1], load_sem.at[6]),
        pltpu.make_async_copy(len_hbm, len_ref, load_sem.at[7]),
        pltpu.make_async_copy(ids_hbm, ids_ref, load_sem.at[8]),
    ]
    for load in loads[:2] + loads[5:] + loads[2:5]:
        load.start()

    barrier = pltpu.get_barrier_semaphore()
    pl.semaphore_signal(barrier, inc=1, device_id=(1 - group, me), device_id_type=MESH)
    for j in range(1, n):
        pl.semaphore_signal(barrier, inc=1, device_id=(group, xor(me, j)), device_id_type=MESH)

    loads[0].wait()
    loads[1].wait()
    pl.semaphore_wait(barrier, n)

    gathers = []
    own, other = group, 1 - group

    half = shard // 2

    def send(slot_mask, piece, part, to):
        slot = xor(me, slot_mask)
        rows = pl.ds(part * half, half)
        copy = pltpu.make_async_remote_copy(
            src_ref=g.at[slot, piece, rows], dst_ref=g.at[slot, piece, rows],
            send_sem=gs_sem.at[len(gathers)], recv_sem=gr_sem.at[slot, piece, part],
            device_id=to, device_id_type=MESH,
        )
        copy.start()
        gathers.append(copy)

    def arrived(slot_mask, piece, part):
        slot = xor(me, slot_mask)
        rows = pl.ds(part * half, half)
        pltpu.make_async_remote_copy(
            src_ref=g.at[slot, piece, rows], dst_ref=g.at[slot, piece, rows],
            send_sem=gs_sem.at[0], recv_sem=gr_sem.at[slot, piece, part],
            device_id=(group, xor(me, 1)), device_id_type=MESH,
        ).wait_recv()

    def peer(mask):
        return (group, xor(me, mask))

    sibling, twin = peer(1), (other, me)
    fasts = [2 * b for b in range(1, fast)]
    slows = [2 * fast * a for a in range(1, slow)]
    early = slows[:1]
    for mask in fasts + slows:
        for part in range(2):
            send(0, own, part, peer(mask))
    for part in range(2):
        for mask in fasts:
            send(0, other, part, peer(mask))
        send(0, own, part, sibling)
        send(0, other, part, sibling)

    for load in loads[5:]:
        load.wait()
    for s in range(seqs):
        idbuf[me, s : s + 1] = jnp.full((1, idbuf.shape[2]), ids_ref[s], jnp.int32)
    k[0] = start_factor(k[0])
    k[1] = start_factor(k[1])
    tail = bank.shape[0] - bank_ref.shape[0]
    if tail:
        bank[bank_ref.shape[0] :] = jnp.zeros((tail, bank.shape[1]), BF16)
    if block > seqs * per:
        wsend[...] = jnp.zeros_like(wsend)

    id_copies = []
    for j in range(1, n):
        copy = pltpu.make_async_remote_copy(
            src_ref=idbuf.at[me], dst_ref=idbuf.at[me],
            send_sem=is_sem.at[j], recv_sem=ir_sem.at[j],
            device_id=(group, xor(me, j)), device_id_type=MESH,
        )
        copy.start()
        id_copies.append(copy)

    def from_slow(mask, part):
        arrived(mask, own, part)
        for b in fasts:
            send(mask, own, part, peer(b))
        send(mask, own, part, twin)
        send(mask, own, part, sibling)

    def from_fast(mask, part):
        for b in fasts:
            arrived(mask + b, own, part)
            if mask and mask not in early:
                send(mask + b, own, part, twin)
            send(mask + b, own, part, sibling)

    def from_twin(mask, part):
        arrived(mask, other, part)
        if mask in early:
            for b in fasts:
                send(mask, other, part, peer(b))
        send(mask, other, part, sibling)

    def last(mask, part):
        for b in fasts:
            arrived(mask + b, other, part)
            send(mask + b, other, part, sibling)

    span = n // slow * shard

    def project(mask, part):
        if part == 0:
            return
        if mask == 0:
            loads[2].wait()
            loads[3].wait()
        for b in [0] + fasts:
            for piece in (own, other):
                for at in range(2):
                    arrived(mask + b + 1, piece, at)
        block_at = xor(me // (2 * fast), mask // (2 * fast))
        columns = pl.ds(pl.multiple_of(block_at * span, 128), span)
        shards = pl.ds(block_at * 2 * fast, 2 * fast)
        x_part = jnp.dot(
            act[:, columns], g[shards, 0].reshape(span, rank), preferred_element_type=F32
        )
        d_part = jnp.dot(
            og[:, columns], g[shards, 1].reshape(span, rank), preferred_element_type=F32
        )
        if mask == 0:
            x_full[...] = x_part
            d_full[...] = d_part
        else:
            x_full[...] += x_part
            d_full[...] += d_part

    events = []
    for a in range(slow):
        if a + 1 < slow:
            events.append((from_slow, slows[a]))
        if a + 2 == slow:
            events.append((project, 0))
        if a:
            events.append((from_twin, slows[a - 1]))
            events.append((from_fast, slows[a - 1]))
            if a > 1:
                events.append((last, slows[a - 2]))
            if a > 2:
                events.append((project, slows[a - 3]))
        else:
            events.append((from_fast, 0))
            if slow > 1:
                events.append((last, 0))
    events.append((last, slows[-1] if slows else 0))
    if slow == 1:
        events.append((project, 0))
    for mask in slows[max(0, slow - 3):]:
        events.append((project, mask))

    panels = rank // PANEL

    def step(_, carry):
        first, second = k[0], k[1]
        k[0] = eliminate_panel(first)
        k[1] = eliminate_panel(second)
        return carry

    steps = [(event, mask, part) for event, mask in events for part in range(2)]
    first, busy = panels // 4, max(1, 3 * len(steps) // 4)
    done = 0
    for at, (event, mask, part) in enumerate(steps):
        upto = min(panels, first + (panels - first) * at // busy)
        if upto > done:
            lax.fori_loop(0, upto - done, step, 0)
            done = upto
        event(mask, part)
    if panels > done:
        lax.fori_loop(0, panels - done, step, 0)

    position = lax.broadcasted_iota(jnp.int32, (length, 1), 0)
    for s in range(seqs):
        rows = slice(s * length, (s + 1) * length)
        valid = (position < len_ref[s]).astype(F32)
        x_proj = (x_full[rows] * valid).astype(BF16)
        d_proj = d_full[rows].astype(BF16)
        grads = lax.dot_general(d_proj, x_proj, (((0,), (0,)), ((), ())), preferred_element_type=F32)
        left = jnp.dot(k[1], grads, precision=lax.Precision.HIGHEST, preferred_element_type=F32)
        white = jnp.dot(left, k[0], precision=lax.Precision.HIGHEST, preferred_element_type=F32)
        wsend[:, s * per : (s + 1) * per] = white.reshape(n, per, rank)

    def exchange(src, dst, send_sem, recv_sem, j):
        copy = pltpu.make_async_remote_copy(
            src_ref=src, dst_ref=dst,
            send_sem=send_sem.at[j], recv_sem=recv_sem.at[j],
            device_id=(group, xor(me, j)), device_id_type=MESH,
        )
        copy.start()
        return copy

    mine = pl.ds(pl.multiple_of(me * block, block), block)
    white_copies = [
        exchange(wsend.at[xor(me, j)], wrecv.at[mine], ws_sem, wr_sem, j) for j in range(n - 1, 0, -1)
    ]
    wrecv[mine] = wsend[me]
    loads[4].wait()
    for copy in white_copies:
        copy.wait_recv()
    for copy in id_copies:
        copy.wait_recv()

    columns = jnp.concatenate(
        [
            jnp.concatenate(
                [wrecv[pl.ds(s * per + a, n, stride=block), :] for s in range(seqs)], axis=0
            ).astype(BF16)
            for a in range(per)
        ],
        axis=1,
    )

    def partial(target):
        rows = bank[pl.ds(pl.multiple_of(target * queries, queries), psend.shape[2])]
        return lax.dot_general(columns, rows, (((1,), (1,)), ((), ())), preferred_element_type=F32)

    score_copies = []
    for j in range(n - 1, 0, -1):
        psend[j] = partial(xor(me, j)).astype(BF16)
        score_copies.append(exchange(psend.at[j], precv.at[j], ps_sem, pr_sem, j))
    total = partial(me)
    ids = jnp.concatenate([idbuf[:, s, :] for s in range(seqs)], axis=0)[:, :1]
    held = n * seqs
    one_hot = (ids == lax.broadcasted_iota(jnp.int32, (held, held), 1)).astype(BF16)
    for copy in score_copies:
        copy.wait_recv()
    for j in range(n - 1, 0, -1):
        total += precv[j].astype(F32)
    placed = lax.dot_general(
        one_hot, total.astype(BF16), (((0,), (0,)), ((), ())), preferred_element_type=F32
    )
    out_ref[...] = placed[:, :queries].astype(BF16)
    for copy in gathers + id_copies + white_copies + score_copies:
        copy.wait_send()


def solution(mesh):
    n = mesh.shape["coord"]
    assert mesh.shape["groups"] == 2
    chips = n // 2
    slow = 1
    while slow * slow < chips:
        slow *= 2
    fast = chips // slow

    def body(activations, out_grads, proj_in, proj_out, cov_in, cov_out, lengths, seq_ids, bank):
        seqs, length, width = activations.shape
        shard, rank = proj_in.shape
        per = bank.shape[1] // rank
        queries = bank.shape[0] // n
        wide = -(-queries // 128) * 128
        block = -(-(seqs * per) // 8) * 8
        held = n * seqs
        vmem = pl.BlockSpec(memory_space=pltpu.VMEM)
        hbm = pl.BlockSpec(memory_space=pl.ANY)
        dma = pltpu.SemaphoreType.DMA
        return pl.pallas_call(
            functools.partial(kernel, n, slow, fast),
            out_shape=jax.ShapeDtypeStruct((held, queries), BF16),
            in_specs=[hbm] * 9,
            out_specs=vmem,
            scratch_shapes=[
                pltpu.SMEM((seqs,), jnp.int32),
                pltpu.SMEM((seqs,), jnp.int32),
                pltpu.VMEM((seqs * length, width), BF16),
                pltpu.VMEM((seqs * length, width), BF16),
                pltpu.VMEM((bank.shape[0] + wide - queries, bank.shape[1]), BF16),
                pltpu.VMEM((n, 2, shard, rank), BF16),
                pltpu.VMEM((2, rank, rank), F32),
                pltpu.VMEM((seqs * length, rank), F32),
                pltpu.VMEM((seqs * length, rank), F32),
                pltpu.VMEM((n, seqs, 128), jnp.int32),
                pltpu.VMEM((n, block, rank), F32),
                pltpu.VMEM((n * block, rank), F32),
                pltpu.VMEM((n, held, wide), BF16),
                pltpu.VMEM((n, held, wide), BF16),
                dma((9,)),
                dma((4 * n,)), dma((n, 2, 2)), dma((n,)), dma((n,)),
                dma((n,)), dma((n,)), dma((n,)), dma((n,)),
            ],
            compiler_params=pltpu.CompilerParams(collective_id=0, has_side_effects=True),
        )(
            activations.reshape(seqs * length, width), out_grads.reshape(seqs * length, width),
            proj_in, proj_out, cov_in, cov_out, lengths, seq_ids, bank,
        )

    in_specs = (
        P(("groups", "coord"), None, None),
        P(("groups", "coord"), None, None),
        P("coord", None),
        P("coord", None),
        P(),
        P(),
        P(("groups", "coord")),
        P(("groups", "coord")),
        P(None, "coord"),
    )
    return jax.shard_map(body, mesh=mesh, in_specs=in_specs, out_specs=P("groups", "coord"), check_vma=False)
```
